512 devices in a mesh: gx: 8 (over x, core), gy: 8 (over z), gz: 8 (over y).
Axes of the slice: x: 4, y: 8, z: 8, core: 2. Of those that a mesh axis runs over, the one named last changes fastest.
Arguments:
- features: float32 [32, 262144], P(None, ('gx', 'gy', 'gz')), may hold values from -6 to 6
- edge_lists: int32 [2, 1048576], P(None, ('gx', 'gy', 'gz')), may hold values from 0 to 512, as said below
- peer_nodes: int32 [27, 16384], P(None, ('gx', 'gy', 'gz')), may hold values from 0 to 512, as said below
- edge_in: float32 [2, 32, 64], replicated, may hold values from -0.75 to 0.75
- edge_out: float32 [2, 32, 32], replicated, may hold values from -1 to 1
- node_in: float32 [2, 32, 64], replicated, may hold values from -0.75 to 0.75
- node_out: float32 [2, 32, 32], replicated, may hold values from -1 to 1
- cotangent: float32 [32, 262144], P(None, ('gx', 'gy', 'gz')), may hold values from -6 to 6
Outputs:
- updated: float32 [32, 262144], P(None, ('gx', 'gy', 'gz'))
- feature_grad: float32 [32, 262144], P(None, ('gx', 'gy', 'gz'))
The draws below stay inside these ranges and needn't reach their ends.
Inputs may be any that keep to these rules, and one draw needn't show every extreme that they name: `edge_lists`: row 0 holds sources and row 1 targets. 512 marks an empty edge in both rows; each device's live edges come first, from two fifths of its 2048 slots to all of them, and some device has all live. `peer_nodes`: row k of a device's block lists its nodes coincident with nodes of the device at grid offset (k // 9 - 1, k // 3 % 3 - 1, k % 3 - 1); 512 marks an empty slot and filled slots come first. Slot s of row k and slot s of that neighbour's row 26 - k are filled together and name the same coincident node. No index repeats within a device's block. Row 13 and rows toward devices outside the grid are empty. Rows toward face neighbours fill 32 // 4 to 32 slots, and some pair fills 32; rows toward edge and corner neighbours fill at most 4 slots, and some pair fills 4.
All inputs are finite; a program needn't handle non-finite values.
Results may differ from the reference program's by a relative error of at most 0.0001.
Values sent between devices are 32-bit elements; how exact they have to be, the bound alone decides.
A program may use at most 64 MiB of HBM per device.

```python
from functools import partial
import jax
import jax.numpy as jnp
import numpy as np
from jax import lax

F = 32
LAYERS = 2
NODES = 512
EDGES = 2048
SLOT = 32
RIM = 4
ALL_NODES = 262144
N_GX = 8
N_GY = 8
N_GZ = 8


def link_offsets():
    return [(link_index // 9 - 1, link_index // 3 % 3 - 1, link_index % 3 - 1) for link_index in range(27)]


def forced_link(select_key, candidates, grid_shape):
    offsets = jnp.asarray(np.array(link_offsets(), dtype=np.int32))
    pick_key, place_key = jax.random.split(select_key)
    table = jnp.asarray(np.array(candidates, dtype=np.int32))
    chosen = table[jax.random.randint(pick_key, (), 0, len(candidates))]
    offset = offsets[chosen]
    lowest = jnp.maximum(-offset, 0)
    highest = jnp.asarray(np.array(grid_shape, dtype=np.int32)) - jnp.maximum(offset, 0)
    place = jax.random.randint(place_key, (3,), lowest, highest)
    return (chosen, place)


def draw_peer_nodes(key, part):
    grid_shape = (N_GX, N_GY, N_GZ)
    device_count = N_GX * N_GY * N_GZ
    base_key = jax.random.fold_in(key, 7)
    face_key, rim_key, first_key, second_key, order_key = jax.random.split(base_key, 5)
    offsets = link_offsets()
    classes = np.array([sum((1 for component in offset if component != 0)) for offset in offsets])
    face_counts = jax.random.randint(face_key, grid_shape + (27,), SLOT // 4, SLOT + 1)
    rim_counts = jax.random.randint(rim_key, grid_shape + (27,), 0, RIM + 1)
    counts = jnp.where(jnp.asarray(classes == 1), face_counts, rim_counts).astype(jnp.int32)
    face_links = [link_index for link_index in range(14, 27) if classes[link_index] == 1]
    rim_links = [link_index for link_index in range(14, 27) if classes[link_index] > 1]
    face_link, face_place = forced_link(first_key, face_links, grid_shape)
    rim_link, rim_place = forced_link(second_key, rim_links, grid_shape)
    counts = counts.at[face_place[0], face_place[1], face_place[2], face_link].set(SLOT)
    counts = counts.at[rim_place[0], rim_place[1], rim_place[2], rim_link].set(RIM)
    coords = [lax.broadcasted_iota(jnp.int32, grid_shape, axis_index) for axis_index in range(3)]
    padded_counts = jnp.pad(counts, ((1, 1), (1, 1), (1, 1), (0, 0)))
    columns = []
    for link_index, offset in enumerate(offsets):
        if link_index > 13:
            inside = jnp.ones(grid_shape, jnp.bool_)
            for axis_index in range(3):
                moved = coords[axis_index] + offset[axis_index]
                inside = inside & (moved >= 0) & (moved < grid_shape[axis_index])
            columns.append(jnp.where(inside, counts[..., link_index], 0))
        elif link_index == 13:
            columns.append(jnp.zeros(grid_shape, jnp.int32))
        else:
            columns.append(padded_counts[1 + offset[0]:1 + offset[0] + N_GX, 1 + offset[1]:1 + offset[1] + N_GY, 1 + offset[2]:1 + offset[2] + N_GZ, 26 - link_index])
    counts_all = jnp.stack(columns, axis=-1).reshape(device_count, 27)
    starts = []
    spans = []
    position = 0
    for link_index in range(27):
        if link_index == 13:
            span = 0
        elif classes[link_index] == 1:
            span = SLOT
        else:
            span = RIM
        starts.append(position)
        spans.append(max(span, 1))
        position = position + span
    start_table = jnp.asarray(np.array(starts, dtype=np.int32))[:, None]
    span_table = jnp.asarray(np.array(spans, dtype=np.int32))[:, None]
    slot_row = lax.broadcasted_iota(jnp.int32, (27, SLOT), 1)
    pick_index = start_table + jnp.minimum(slot_row, span_table - 1)
    order_keys = jax.random.split(order_key, device_count)
    orders = jax.vmap(lambda one_key: jax.random.permutation(one_key, NODES))(order_keys).astype(jnp.int32)
    chosen = jnp.take(orders, pick_index.reshape(-1), axis=1).reshape(device_count, 27, SLOT)
    slot_index = lax.broadcasted_iota(jnp.int32, (device_count, 27, SLOT), 2)
    lists = jnp.where(slot_index < counts_all[:, :, None], chosen, NODES)
    return lists.transpose(1, 0, 2).reshape(27, device_count * SLOT).astype(jnp.int32)


def draw_edge_lists(key, part):
    device_count = N_GX * N_GY * N_GZ
    base_key = jax.random.fold_in(key, 11)
    live_key, pick_key, source_key, stride_key = jax.random.split(base_key, 4)
    live = jax.random.randint(live_key, (device_count,), 2 * EDGES // 5, EDGES + 1)
    full_device = jax.random.randint(pick_key, (), 0, device_count)
    live = jnp.where(lax.broadcasted_iota(jnp.int32, (device_count,), 0) == full_device, EDGES, live)
    sources = jax.random.randint(source_key, (device_count, EDGES), 0, NODES)
    strides = jax.random.randint(stride_key, (device_count, EDGES), 1, 33)
    targets = (sources + strides) % NODES
    slot_index = lax.broadcasted_iota(jnp.int32, (device_count, EDGES), 1)
    used = slot_index < live[:, None]
    sources = jnp.where(used, sources, NODES)
    targets = jnp.where(used, targets, NODES)
    return jnp.stack([sources, targets]).reshape(2, device_count * EDGES).astype(jnp.int32)


def levels(rng, shape, cuts, low, top_value):
    factor_of = 1.0
    for axis_at, parts in cuts:
        steps = jax.random.uniform(jax.random.fold_in(jax.random.fold_in(rng, 6), axis_at), (parts,), jnp.float32, low / len(cuts), top_value / len(cuts))
        factor_of = factor_of * jnp.repeat(jnp.exp(steps), shape[axis_at] // parts).reshape((-1,) + (1,) * (len(shape) - 1 - axis_at))
    return factor_of


def normal_values(stream_key, dims, scale, bound, pieces=(), kind=jnp.bfloat16):
    level = levels(stream_key, dims, pieces, -0.22, 0.18) if pieces else 1.0
    drawn = jax.random.normal(stream_key, dims, jnp.float32) * scale * level
    return jnp.minimum(jnp.maximum(drawn, -bound), bound).astype(kind)


def setup_inputs(seed: int = 0) -> dict:
    splits = jax.random.split(jax.random.key(seed), 9)
    return {
        "features": normal_values(splits[0], (F, ALL_NODES), 1.0, 6.0, ((1, 512),), jnp.float32),
        "edge_lists": draw_edge_lists(jax.random.fold_in(splits[8], 71), 0),
        "peer_nodes": draw_peer_nodes(jax.random.fold_in(splits[8], 71), 0),
        "edge_in": normal_values(splits[3], (LAYERS, F, 2 * F), (2 * F) ** -0.5, 0.75, (), jnp.float32),
        "edge_out": normal_values(splits[4], (LAYERS, F, F), F ** -0.5, 1.0, (), jnp.float32),
        "node_in": normal_values(splits[5], (LAYERS, F, 2 * F), (2 * F) ** -0.5, 0.75, (), jnp.float32),
        "node_out": normal_values(splits[6], (LAYERS, F, F), F ** -0.5, 1.0, (), jnp.float32),
        "cotangent": normal_values(splits[7], (F, ALL_NODES), 1.0, 6.0, ((1, 512),), jnp.float32),
    }


def link_table():
    return [(link_index // 9 - 1, link_index // 3 % 3 - 1, link_index % 3 - 1) for link_index in range(27)]

def with_zero(columns):
    return jnp.concatenate([columns, jnp.zeros(columns.shape[:-1] + (1,), columns.dtype)], axis=-1)

def matmul(left, right):
    return jnp.dot(left, right, precision=lax.Precision.HIGHEST)

def local_partial(field, sources, targets, edge_first, edge_second):
    width = field.shape[0]
    extended = with_zero(field)
    from_source = jnp.take(extended, sources, axis=1)
    from_target = jnp.take(extended, targets, axis=1)
    edge_pre = matmul(edge_first[:, :width], from_source) + matmul(edge_first[:, width:], from_target)
    messages = matmul(edge_second, jax.nn.silu(edge_pre))
    return jnp.zeros_like(extended).at[:, targets].add(messages)[:, :-1]

def take_lists(node_rows, link_lists):
    return jnp.take(node_rows, link_lists, axis=1)

def add_lists(node_rows, link_lists, arrivals):
    return node_rows.at[:, link_lists.reshape(-1)].add(arrivals)

def assemble_all(partials, lists):
    device_count = partials.shape[0]
    width = partials.shape[1]
    slots = lists.shape[2]
    extended = with_zero(partials)
    outgoing = jax.vmap(take_lists)(extended, lists)
    grid = outgoing.reshape(N_GX, N_GY, N_GZ, width, 27, slots)
    border = jnp.pad(grid, ((1, 1), (1, 1), (1, 1), (0, 0), (0, 0), (0, 0)))
    incoming = []
    for link_index, offset in enumerate(link_table()):
        incoming.append(border[1 + offset[0]:1 + offset[0] + N_GX, 1 + offset[1]:1 + offset[1] + N_GY, 1 + offset[2]:1 + offset[2] + N_GZ, :, 26 - link_index])
    incoming = jnp.stack(incoming, axis=4).reshape(device_count, width, 27 * slots)
    summed = jax.vmap(add_lists)(extended, lists, incoming)
    return summed[:, :, :-1]

def forward(features, edge_lists, peer_nodes, edge_in, edge_out, node_in, node_out):
    width = features.shape[0]
    device_count = N_GX * N_GY * N_GZ
    field = features.reshape(width, device_count, NODES).transpose(1, 0, 2)
    sources = edge_lists[0].reshape(device_count, EDGES)
    targets = edge_lists[1].reshape(device_count, EDGES)
    lists = peer_nodes.reshape(27, device_count, SLOT).transpose(1, 0, 2)
    for layer_index in range(LAYERS):
        edge_first = edge_in[layer_index]
        edge_second = edge_out[layer_index]

        def partial_of(items):
            return local_partial(items[0], items[1], items[2], edge_first, edge_second)
        partials = lax.map(partial_of, (field, sources, targets))
        aggregate = assemble_all(partials, lists)
        node_first = node_in[layer_index]
        node_pre = jnp.einsum('of,dfn->don', node_first[:, :width], field, precision=lax.Precision.HIGHEST)
        node_pre = node_pre + jnp.einsum('of,dfn->don', node_first[:, width:], aggregate, precision=lax.Precision.HIGHEST)
        field = field + jnp.einsum('of,dfn->don', node_out[layer_index], jax.nn.silu(node_pre), precision=lax.Precision.HIGHEST)
    return field.transpose(1, 0, 2).reshape(width, device_count * NODES)

def reference(features, edge_lists, peer_nodes, edge_in, edge_out, node_in, node_out, cotangent):
    closed = partial(forward, edge_lists=edge_lists, peer_nodes=peer_nodes, edge_in=edge_in, edge_out=edge_out, node_in=node_in, node_out=node_out)
    updated, pullback = jax.vjp(closed, features)
    feature_grad = pullback(cotangent)[0]
    return (updated, feature_grad)
```

```python
import functools

import jax
import jax.numpy as jnp
from jax import lax
from jax.experimental import pallas as pl
from jax.experimental.pallas import tpu as pltpu
from jax.sharding import PartitionSpec as P

F = 32
LANES = 128
AXES = ("gx", "gy", "gz")
LINKS = [(k // 9 - 1, k // 3 % 3 - 1, k % 3 - 1) for k in range(27)]
REACH = [sum(abs(c) for c in offset) for offset in LINKS]
FACES = [k for k in range(27) if REACH[k] == 1]
RIMS = [k for k in range(27) if REACH[k] > 1]
ORDER = sorted(RIMS, key=lambda k: -REACH[k]) + FACES
RIM_ROW = 8 * len(FACES)
ROWS = 80
f32, bf16, i32 = jnp.float32, jnp.bfloat16, jnp.int32


def split(value):
    high = value.astype(bf16)
    low = (value - high.astype(f32)).astype(bf16)
    return high, low


def dot(left, right):
    return lax.dot_general(left, right, (((1,), (0,)), ((), ())), preferred_element_type=f32)


def spread(matrix):
    rows = matrix.shape[0]
    wide = jnp.concatenate([matrix] * (LANES // matrix.shape[1]), axis=1)
    high, low = split(0.5 * wide)
    return jnp.where(iota((rows, LANES), 1) < LANES // 2, high.astype(f32), low.astype(f32)).astype(bf16)


def spread_flipped(matrix):
    rows = matrix.shape[0]
    tall = jnp.concatenate([matrix] * (LANES // rows), axis=0)
    wide = jnp.transpose(jnp.concatenate([tall, jnp.zeros((LANES, LANES - F), f32)], axis=1))[:F]
    high, low = split(0.5 * wide)
    if rows == 64:
        return jnp.concatenate([high, low], axis=1)
    return jnp.where(iota((F, LANES), 1) < LANES // 2, high.astype(f32), low.astype(f32)).astype(bf16)


def times(weights, value):
    high, low = split(value)
    return 2.0 * dot(weights, jnp.concatenate([high, low, high, low], axis=0))


def sigmoid_of(value):
    return 0.5 * jnp.tanh(0.5 * value) + 0.5


def lane_take(chunk, index):
    return jnp.take_along_axis(chunk, index, axis=1, mode="promise_in_bounds")


def iota(shape, dim):
    return lax.broadcasted_iota(i32, shape, dim)


def take(table, index):
    rows = table.shape[0]
    index = jnp.broadcast_to(index, (8, LANES))
    lane, part = index & (LANES - 1), index >> 7
    pieces = []
    for top in range(0, rows, 8):
        total = jnp.zeros((8, LANES), f32)
        for chunk in range(table.shape[1] // LANES):
            got = lane_take(table[top : top + 8, chunk * LANES : (chunk + 1) * LANES], lane)
            total = jnp.where(part == chunk, got, total)
        pieces.append(total)
    return jnp.concatenate(pieces, axis=0)


def kernel(
    sizes, x_ref, edges_ref, peers_ref, edge_in_ref, edge_out_ref, node_in_ref, node_out_ref, cot_ref,
    updated_ref, grad_ref,
    hot_target, hot_source, slopes, masked, peer_pad, held,
    face_out, rim_out, face_in, rim_in, send_sem, recv_sem,
):
    here = [lax.axis_index(axis) for axis in AXES]
    nodes = x_ref.shape[1]
    edges = edges_ref.shape[1]
    blocks = edges // LANES
    chunks = nodes // LANES

    def there(k):
        inside = True
        for place, step, size in zip(here, LINKS[k], sizes):
            if step < 0:
                inside = inside & (place > 0)
            elif step > 0:
                inside = inside & (place < size - 1)
        return inside

    def device(k):
        return tuple(place + step for place, step in zip(here, LINKS[k]))

    def copy(turn, k):
        if REACH[k] == 1:
            source = face_out.at[turn, FACES.index(k)]
            target = face_in.at[turn, FACES.index(26 - k)]
        else:
            source = rim_out.at[turn, k]
            target = rim_in.at[turn, 26 - k]
        return pltpu.make_async_remote_copy(
            src_ref=source, dst_ref=target, send_sem=send_sem.at[turn, k], recv_sem=recv_sem.at[turn, 26 - k],
            device_id=device(k), device_id_type=pl.DeviceIdType.MESH,
        )

    barrier = pltpu.get_barrier_semaphore()
    present = jnp.int32(0)
    for k in ORDER:
        present = present + jnp.where(there(k), 1, 0).astype(i32)

        @pl.when(there(k))
        def _():
            pl.semaphore_signal(barrier, inc=1, device_id=device(k), device_id_type=pl.DeviceIdType.MESH)

    def source_of(block):
        return edges_ref[0:1, block * LANES : (block + 1) * LANES]

    def target_of(block):
        return edges_ref[1:2, block * LANES : (block + 1) * LANES]

    def build_hot(hot, index_of):
        row = iota((256, LANES), 0)
        for block in range(blocks):
            index = jnp.broadcast_to(index_of(block) & 255, (256, LANES))
            hot[:, block * LANES : (block + 1) * LANES] = jnp.where(row == index, 1.0, 0.0).astype(bf16)

    peer_pad[...] = jnp.full(peer_pad.shape, 512, i32)
    peer_pad[0:27, 0 : peers_ref.shape[1]] = peers_ref[...]
    lane = iota((8, LANES), 1)
    group = iota((8, LANES), 0)
    by_slot = jnp.transpose(peer_pad[...].astype(f32)).astype(i32)[0:8]
    rim_index = lane - RIM_ROW
    slot_node = lane_take(by_slot, jnp.maximum(rim_index, 0))
    keep = jnp.zeros((8, LANES), jnp.bool_)
    for k in RIMS:
        keep = keep | (rim_index == k)
    slot_node = jnp.where(keep & (group < 4), slot_node, 512)
    for p, k in enumerate(FACES):
        row = jnp.broadcast_to(peer_pad[k : k + 1, :], (8, LANES))
        got = lane_take(row, 8 * group + (lane & 7))
        slot_node = jnp.where(lane >> 3 == p, got, slot_node)

    def node_slots():
        padded = jnp.concatenate([slot_node, jnp.full((LANES - 8, LANES), 512, i32)], axis=0)
        by_row = jnp.transpose(padded.astype(f32)).astype(i32)[0:ROWS]
        rows = iota((ROWS, LANES), 0)
        codes = []
        for chunk in range(chunks):
            node = iota((ROWS, LANES), 1) + chunk * LANES
            code = jnp.zeros((ROWS, LANES), f32)
            for g in range(4):
                column = jnp.broadcast_to(by_row[:, g : g + 1], (ROWS, LANES))
                code = code + jnp.where(column == node, rows + (LANES * g + 1), 0).astype(f32)
            codes.append(jnp.sum(code, axis=0, keepdims=True).astype(i32))
        return codes

    def pack(turn, field):
        columns = [take(field, slot_node[g : g + 1]) for g in range(4)]
        packed = jnp.transpose(jnp.concatenate(columns, axis=0))
        for p in range(len(FACES)):
            face_out[turn, p] = packed[8 * p : 8 * p + 8]
        for k in RIMS:
            rim_out[turn, k] = packed[RIM_ROW + k : RIM_ROW + k + 1]

    def send(turn):
        for k in ORDER:

            @pl.when(there(k))
            def _():
                copy(turn, k).start()

    def receive(turn):
        for k in FACES + RIMS[::-1]:

            @pl.when(there(k))
            def _():
                copy(turn, 26 - k).wait_recv()

    def unpack(turn, codes):
        faces = face_in[turn].reshape(RIM_ROW, LANES)
        rims = rim_in[turn].reshape(rim_in.shape[1], LANES)
        arrived = jnp.concatenate([faces, rims], axis=0)
        arrived = jnp.concatenate([arrived, jnp.zeros((LANES - arrived.shape[0], LANES), f32)], axis=0)
        columns = jnp.transpose(arrived)
        pieces = []
        for chunk in range(chunks):
            code = jnp.broadcast_to(codes[chunk] - 1, (8, LANES))
            row, which = code & (LANES - 1), code >> 7
            tops = []
            for top in range(0, F, 8):
                total = jnp.zeros((8, LANES), f32)
                for g in range(4):
                    got = lane_take(columns[F * g + top : F * g + top + 8], row)
                    total = jnp.where(which == g, got, total)
                tops.append(total)
            pieces.append(jnp.concatenate(tops, axis=0))
        return jnp.concatenate(pieces, axis=1)

    def put_masked(block, value, index):
        half = jnp.broadcast_to(index >> 8, (F, LANES))
        columns = slice(block * LANES, (block + 1) * LANES)
        for part in range(2):
            high, low = split(jnp.where(half == part, value, 0.0))
            masked[64 * part : 64 * part + 32, columns] = high
            masked[64 * part + 32 : 64 * part + 64, columns] = low

    def scatter(hot):
        total = lax.dot_general(
            masked[...], hot[...], (((1,), (1,)), ((), ())), preferred_element_type=f32
        )
        return jnp.concatenate([total[0:32] + total[32:64], total[64:96] + total[96:128]], axis=1)

    def edge_forward(layer, table):
        first, second = table[:F], table[F:]
        for block in range(blocks):
            pre = take(first, source_of(block)) + take(second, target_of(block))
            gate = sigmoid_of(pre)
            slopes[layer, :, block * LANES : (block + 1) * LANES] = gate * (1.0 + pre * (1.0 - gate))
            put_masked(block, pre * gate, target_of(block))
        return scatter(hot_target)

    def edge_backward(layer, table):
        deltas = []
        for block in range(blocks):
            delta = take(table, target_of(block)) * slopes[layer, :, block * LANES : (block + 1) * LANES]
            deltas.append(delta)
            put_masked(block, delta, target_of(block))
        to_target = scatter(hot_target)
        for block in range(blocks):
            put_masked(block, deltas[block], source_of(block))
        to_source = scatter(hot_source)
        return jnp.concatenate([to_source, to_target], axis=0)

    ends, joint, own, out, mixed = [], [], [], [], []
    for layer in range(2):
        entry = edge_in_ref[layer]
        node = node_in_ref[layer]
        ends.append(jnp.concatenate([entry[:, :F], entry[:, F:]], axis=0))
        own.append(node[:, :F])
        out.append(node_out_ref[layer])
        wide = jnp.concatenate([edge_out_ref[layer]] * 4, axis=1)
        mixed.append(times(spread(node[:, F:]), wide)[:, :F])

    field = x_ref[...]
    build_hot(hot_target, target_of)
    sums = edge_forward(0, times(spread(ends[0]), field))
    pack(0, sums)
    pl.semaphore_wait(barrier, present)
    send(0)

    codes = node_slots()
    build_hot(hot_source, source_of)
    held[0] = times(spread(own[0]), field)
    receive(0)
    pre = held[0] + times(spread(mixed[0]), sums + unpack(0, codes))
    gate = sigmoid_of(pre)
    node_slope = gate * (1.0 + pre * (1.0 - gate))
    field = field + times(spread(out[0]), pre * gate)

    sums = edge_forward(1, times(spread(ends[1]), field))
    pack(1, sums)
    send(1)
    held[1] = times(spread(own[1]), field)
    cot = cot_ref[...]
    lifted = times(spread_flipped(out[1]), cot)
    receive(1)
    pre = held[1] + times(spread(mixed[1]), sums + unpack(1, codes))
    gate = sigmoid_of(pre)

    delta = lifted * (gate * (1.0 + pre * (1.0 - gate)))
    sums = times(spread_flipped(mixed[1]), delta)
    pack(2, sums)
    send(2)
    updated_ref[...] = field + times(spread(out[1]), pre * gate)
    held[2] = cot + times(spread_flipped(own[1]), delta)
    receive(2)
    both = edge_backward(1, sums + unpack(2, codes))
    upstream = held[2] + times(spread_flipped(ends[1]), both)
    delta = times(spread_flipped(out[0]), upstream) * node_slope
    sums = times(spread_flipped(mixed[0]), delta)
    pack(3, sums)
    send(3)
    held[3] = upstream + times(spread_flipped(own[0]), delta)
    receive(3)
    both = edge_backward(0, sums + unpack(3, codes))
    grad_ref[...] = held[3] + times(spread_flipped(ends[0]), both)

    for turn in range(4):
        for k in ORDER:

            @pl.when(there(k))
            def _():
                copy(turn, k).wait_send()


def solution(mesh):
    sizes = tuple(mesh.shape[axis] for axis in AXES)

    def on_device(features, edge_lists, peer_nodes, edge_in, edge_out, node_in, node_out, cotangent):
        nodes = features.shape[1]
        edges = edge_lists.shape[1]
        vmem = pl.BlockSpec(memory_space=pltpu.VMEM)
        return pl.pallas_call(
            functools.partial(kernel, sizes),
            out_shape=(jax.ShapeDtypeStruct(features.shape, f32), jax.ShapeDtypeStruct(features.shape, f32)),
            in_specs=[vmem] * 8,
            out_specs=(vmem, vmem),
            scratch_shapes=[
                pltpu.VMEM((256, edges), bf16),
                pltpu.VMEM((256, edges), bf16),
                pltpu.VMEM((2, F, edges), f32),
                pltpu.VMEM((128, edges), bf16),
                pltpu.VMEM((LANES, LANES), i32),
                pltpu.VMEM((4, F, nodes), f32),
                pltpu.VMEM((4, len(FACES), 8, LANES), f32),
                pltpu.VMEM((4, 27, 1, LANES), f32),
                pltpu.VMEM((4, len(FACES), 8, LANES), f32),
                pltpu.VMEM((4, 27, 1, LANES), f32),
                pltpu.SemaphoreType.DMA((4, 27)),
                pltpu.SemaphoreType.DMA((4, 27)),
            ],
            compiler_params=pltpu.CompilerParams(collective_id=0, has_side_effects=True),
        )(features, edge_lists, peer_nodes, edge_in, edge_out, node_in, node_out, cotangent)

    split_columns = P(None, AXES)
    return jax.shard_map(
        on_device,
        mesh=mesh,
        in_specs=(split_columns, split_columns, split_columns, P(), P(), P(), P(), split_columns),
        out_specs=(split_columns, split_columns),
        check_vma=False,
    )
```

```python
import functools

import jax
import jax.numpy as jnp
from jax import lax
from jax.experimental import pallas as pl
from jax.experimental.pallas import tpu as pltpu
from jax.sharding import PartitionSpec as P

F = 32
LANES = 128
AXES = ("gx", "gy", "gz")
LINKS = [(k // 9 - 1, k // 3 % 3 - 1, k % 3 - 1) for k in range(27)]
REACH = [sum(abs(c) for c in offset) for offset in LINKS]
FACES = [k for k in range(27) if REACH[k] == 1]
RIMS = [k for k in range(27) if REACH[k] > 1]
ORDER = sorted(RIMS, key=lambda k: -REACH[k]) + FACES
RIM_ROW = 8 * len(FACES)
ROWS = 80
f32, bf16, i32 = jnp.float32, jnp.bfloat16, jnp.int32


def split(value):
    high = value.astype(bf16)
    low = (value - high.astype(f32)).astype(bf16)
    return high, low


def dot(left, right):
    return lax.dot_general(left, right, (((1,), (0,)), ((), ())), preferred_element_type=f32)


def spread(matrix):
    rows = matrix.shape[0]
    wide = jnp.concatenate([matrix] * (LANES // matrix.shape[1]), axis=1)
    high, low = split(0.5 * wide)
    return jnp.where(iota((rows, LANES), 1) < LANES // 2, high.astype(f32), low.astype(f32)).astype(bf16)


def spread_flipped(matrix):
    rows = matrix.shape[0]
    tall = jnp.concatenate([matrix] * (LANES // rows), axis=0)
    wide = jnp.transpose(jnp.concatenate([tall, jnp.zeros((LANES, LANES - F), f32)], axis=1))[:F]
    high, low = split(0.5 * wide)
    if rows == 64:
        return jnp.concatenate([high, low], axis=1)
    return jnp.where(iota((F, LANES), 1) < LANES // 2, high.astype(f32), low.astype(f32)).astype(bf16)


def times(weights, value):
    high, low = split(value)
    return 2.0 * dot(weights, jnp.concatenate([high, low, high, low], axis=0))


def sigmoid_of(value):
    return 0.5 * jnp.tanh(0.5 * value) + 0.5


def lane_take(chunk, index):
    return jnp.take_along_axis(chunk, index, axis=1, mode="promise_in_bounds")


def iota(shape, dim):
    return lax.broadcasted_iota(i32, shape, dim)


def take(table, index):
    rows = table.shape[0]
    index = jnp.broadcast_to(index, (8, LANES))
    lane, part = index & (LANES - 1), index >> 7
    pieces = []
    for top in range(0, rows, 8):
        total = jnp.zeros((8, LANES), f32)
        for chunk in range(table.shape[1] // LANES):
            got = lane_take(table[top : top + 8, chunk * LANES : (chunk + 1) * LANES], lane)
            total = jnp.where(part == chunk, got, total)
        pieces.append(total)
    return jnp.concatenate(pieces, axis=0)


def kernel(
    sizes, x_hbm, edges_hbm, peers_hbm, edge_in_hbm, edge_out_hbm, node_in_hbm, node_out_hbm, cot_hbm,
    updated_ref, grad_ref,
    x_ref, edges_ref, peers_ref, edge_in_ref, edge_out_ref, node_in_ref, node_out_ref, cot_ref, load_sem,
    hot_target, hot_source, slopes, masked, peer_pad, held, ends_to, small_to, ends_from,
    face_out, rim_out, face_in, rim_in, send_sem, recv_sem,
):
    here = [lax.axis_index(axis) for axis in AXES]
    nodes = x_ref.shape[1]
    edges = edges_ref.shape[1]
    blocks = edges // LANES
    chunks = nodes // LANES

    def there(k):
        inside = None
        for place, step, size in zip(here, LINKS[k], sizes):
            if step:
                ok = place > 0 if step < 0 else place < size - 1
                inside = ok if inside is None else inside & ok
        return inside

    def device(k):
        return tuple(place + step for place, step in zip(here, LINKS[k]))

    def copy(turn, k):
        if REACH[k] == 1:
            source = face_out.at[turn, FACES.index(k)]
            target = face_in.at[turn, FACES.index(26 - k)]
        else:
            source = rim_out.at[turn, k]
            target = rim_in.at[turn, 26 - k]
        return pltpu.make_async_remote_copy(
            src_ref=source, dst_ref=target,
            send_sem=send_sem.at[min(REACH[k], 2) - 1], recv_sem=recv_sem.at[turn, min(REACH[k], 2) - 1],
            device_id=device(k), device_id_type=pl.DeviceIdType.MESH,
        )

    at_rim = jnp.int32(0)
    for place, size in zip(here, sizes):
        at_rim = at_rim + jnp.where((place == 0) | (place == size - 1), 1, 0).astype(i32)
    counts = [(6 - rim, 3 ** (3 - rim) * 2**rim - 7 + rim) for rim in range(4)]

    barrier = pltpu.get_barrier_semaphore()
    for k in ORDER:

        @pl.when(there(k))
        def _():
            pl.semaphore_signal(barrier, inc=1, device_id=device(k), device_id_type=pl.DeviceIdType.MESH)

    loads = [
        pltpu.make_async_copy(source, target, load_sem.at[at])
        for at, (source, target) in enumerate(
            (
                (x_hbm, x_ref), (edge_in_hbm, edge_in_ref), (edges_hbm, edges_ref), (peers_hbm, peers_ref),
                (edge_out_hbm, edge_out_ref), (node_in_hbm, node_in_ref), (node_out_hbm, node_out_ref),
                (cot_hbm, cot_ref),
            )
        )
    ]
    for load in loads:
        load.start()
    for load in loads:
        load.wait()

    def source_of(block):
        return edges_ref[0:1, block * LANES : (block + 1) * LANES]

    def target_of(block):
        return edges_ref[1:2, block * LANES : (block + 1) * LANES]

    def build_hot(hot, index_of):
        row = iota((256, LANES), 0)
        for block in range(blocks):
            index = jnp.broadcast_to(index_of(block) & 255, (256, LANES))
            hot[:, block * LANES : (block + 1) * LANES] = jnp.where(row == index, 1.0, 0.0).astype(bf16)

    peer_pad[...] = jnp.full(peer_pad.shape, 512, i32)
    peer_pad[0:27, 0 : peers_ref.shape[1]] = peers_ref[...]
    lane = iota((8, LANES), 1)
    group = iota((8, LANES), 0)
    by_slot = jnp.transpose(peer_pad[...].astype(f32)).astype(i32)[0:8]
    rim_index = lane - RIM_ROW
    slot_node = lane_take(by_slot, jnp.maximum(rim_index, 0))
    keep = jnp.zeros((8, LANES), jnp.bool_)
    for k in RIMS:
        keep = keep | (rim_index == k)
    slot_node = jnp.where(keep & (group < 4), slot_node, 512)
    for p, k in enumerate(FACES):
        row = jnp.broadcast_to(peer_pad[k : k + 1, :], (8, LANES))
        got = lane_take(row, 8 * group + (lane & 7))
        slot_node = jnp.where(lane >> 3 == p, got, slot_node)

    def node_slots():
        padded = jnp.concatenate([slot_node, jnp.full((LANES - 8, LANES), 512, i32)], axis=0)
        by_row = jnp.transpose(padded.astype(f32)).astype(i32)[0:ROWS]
        rows = iota((ROWS, LANES), 0)
        codes = []
        for chunk in range(chunks):
            node = iota((ROWS, LANES), 1) + chunk * LANES
            code = jnp.zeros((ROWS, LANES), f32)
            for g in range(4):
                column = jnp.broadcast_to(by_row[:, g : g + 1], (ROWS, LANES))
                code = code + jnp.where(column == node, rows + (LANES * g + 1), 0).astype(f32)
            codes.append(jnp.sum(code, axis=0, keepdims=True).astype(i32))
        return codes

    def pack(turn, field):
        columns = [take(field, slot_node[g : g + 1]) for g in range(4)]
        packed = jnp.transpose(jnp.concatenate(columns, axis=0))
        for p in range(len(FACES)):
            face_out[turn, p] = packed[8 * p : 8 * p + 8]
        for k in RIMS:
            rim_out[turn, k] = packed[RIM_ROW + k : RIM_ROW + k + 1]

    def send(turn):
        for k in ORDER:

            @pl.when(there(k))
            def _():
                copy(turn, k).start()

    def receive(turn):
        for rim, (faces, rims) in enumerate(counts):

            @pl.when(at_rim == rim)
            def _():
                landed = ((face_in.at[turn, 0:faces], 0), (rim_in.at[turn, 0:rims], 1))
                for block, which in landed:
                    pltpu.make_async_copy(block, block, recv_sem.at[turn, which]).wait()

    def unpack(turn, codes):
        faces = face_in[turn].reshape(RIM_ROW, LANES)
        rims = rim_in[turn].reshape(rim_in.shape[1], LANES)
        arrived = jnp.concatenate([faces, rims], axis=0)
        arrived = jnp.concatenate([arrived, jnp.zeros((LANES - arrived.shape[0], LANES), f32)], axis=0)
        columns = jnp.transpose(arrived)
        pieces = []
        for chunk in range(chunks):
            code = jnp.broadcast_to(codes[chunk] - 1, (8, LANES))
            row, which = code & (LANES - 1), code >> 7
            tops = []
            for top in range(0, F, 8):
                total = jnp.zeros((8, LANES), f32)
                for g in range(4):
                    got = lane_take(columns[F * g + top : F * g + top + 8], row)
                    total = jnp.where(which == g, got, total)
                tops.append(total)
            pieces.append(jnp.concatenate(tops, axis=0))
        return jnp.concatenate(pieces, axis=1)

    def put_masked(block, value, index):
        half = jnp.broadcast_to(index >> 8, (F, LANES))
        columns = slice(block * LANES, (block + 1) * LANES)
        for part in range(2):
            high, low = split(jnp.where(half == part, value, 0.0))
            masked[64 * part : 64 * part + 32, columns] = high
            masked[64 * part + 32 : 64 * part + 64, columns] = low

    def scatter(hot):
        total = lax.dot_general(
            masked[...], hot[...], (((1,), (1,)), ((), ())), preferred_element_type=f32
        )
        return jnp.concatenate([total[0:32] + total[32:64], total[64:96] + total[96:128]], axis=1)

    def edge_forward(layer, table):
        first, second = table[:F], table[F:]
        for block in range(blocks):
            pre = take(first, source_of(block)) + take(second, target_of(block))
            gate = sigmoid_of(pre)
            slopes[layer, :, block * LANES : (block + 1) * LANES] = gate * (1.0 + pre * (1.0 - gate))
            put_masked(block, pre * gate, target_of(block))
        return scatter(hot_target)

    def slope_sums(layer):
        for block in range(blocks):
            put_masked(block, slopes[layer, :, block * LANES : (block + 1) * LANES], target_of(block))
        return scatter(hot_target)

    def edge_backward(layer, table, summed):
        for block in range(blocks):
            slope = slopes[layer, :, block * LANES : (block + 1) * LANES]
            put_masked(block, take(table, target_of(block)) * slope, source_of(block))
        return jnp.concatenate([scatter(hot_source), table * summed], axis=0)

    def tiled(matrix):
        return jnp.concatenate([matrix] * 4, axis=1)

    own, out, mix, own_back, out_back, mix_back = [2 * at for at in range(6)]
    entry = [jnp.concatenate([edge_in_ref[layer][:, :F], edge_in_ref[layer][:, F:]], axis=0) for layer in range(2)]
    build_hot(hot_target, target_of)
    sums = edge_forward(0, times(spread(entry[0]), x_ref[...]))
    pack(0, sums)
    rim_counts = [f + r for f, r in counts]
    present = jnp.int32(rim_counts[0])
    for rim in range(1, 4):
        present = jnp.where(at_rim == rim, rim_counts[rim], present)
    pl.semaphore_wait(barrier, present)
    send(0)

    for layer in range(2):
        node = node_in_ref[layer]
        mixed = times(spread(node[:, F:]), tiled(edge_out_ref[layer]))[:, :F]
        small_to[own + layer] = spread(node[:, :F])
        small_to[out + layer] = spread(node_out_ref[layer])
        small_to[mix + layer] = spread(mixed)
        small_to[own_back + layer] = spread_flipped(node[:, :F])
        small_to[out_back + layer] = spread_flipped(node_out_ref[layer])
        small_to[mix_back + layer] = spread_flipped(mixed)
        ends_from[layer] = spread_flipped(entry[layer])
    ends_to[0] = spread(entry[1])
    through = times(ends_to[0], tiled(node_out_ref[0]))[:, :F]
    ends_to[1] = spread(through)
    ends_from[2] = spread_flipped(through)
    codes = node_slots()
    build_hot(hot_source, source_of)
    held[4] = slope_sums(0)
    field = x_ref[...]
    held[0] = times(small_to[own], field)
    both_ends = times(ends_to[0], field)
    held[5] = both_ends[:F]
    held[6] = both_ends[F:]
    receive(0)
    pre = held[0] + times(small_to[mix], sums + unpack(0, codes))
    gate = sigmoid_of(pre)
    active = pre * gate
    held[7] = gate * (1.0 + pre * (1.0 - gate))
    table = jnp.concatenate([held[5], held[6]], axis=0) + times(ends_to[1], active)
    sums = edge_forward(1, table)
    pack(1, sums)
    send(1)
    field = field + times(small_to[out], active)
    held[1] = times(small_to[own + 1], field)
    held[8] = times(small_to[out_back + 1], cot_ref[...])
    held[5] = slope_sums(1)
    receive(1)
    pre = held[1] + times(small_to[mix + 1], sums + unpack(1, codes))
    gate = sigmoid_of(pre)

    delta = held[8] * (gate * (1.0 + pre * (1.0 - gate)))
    sums = times(small_to[mix_back + 1], delta)
    pack(2, sums)
    send(2)
    updated_ref[...] = field + times(small_to[out + 1], pre * gate)
    held[2] = cot_ref[...] + times(small_to[own_back + 1], delta)
    held[6] = times(small_to[out_back], held[2])
    receive(2)
    both = edge_backward(1, sums + unpack(2, codes), held[5])
    delta = (held[6] + times(ends_from[2], both)) * held[7]
    sums = times(small_to[mix_back], delta)
    pack(3, sums)
    send(3)
    held[3] = held[2] + times(ends_from[1], both) + times(small_to[own_back], delta)
    receive(3)
    both = edge_backward(0, sums + unpack(3, codes), held[4])
    grad_ref[...] = held[3] + times(ends_from[0], both)

    for rim, (faces, rims) in enumerate(counts):

        @pl.when(at_rim == rim)
        def _():
            for block, which in ((face_out.at[:, 0:faces], 0), (rim_out.at[:, 0:rims], 1)):
                pltpu.make_async_copy(block, block, send_sem.at[which]).wait()


def solution(mesh):
    sizes = tuple(mesh.shape[axis] for axis in AXES)

    def on_device(*operands):
        nodes = operands[0].shape[1]
        edges = operands[1].shape[1]
        anywhere = pl.BlockSpec(memory_space=pl.ANY)
        vmem = pl.BlockSpec(memory_space=pltpu.VMEM)
        return pl.pallas_call(
            functools.partial(kernel, sizes),
            out_shape=(jax.ShapeDtypeStruct((F, nodes), f32), jax.ShapeDtypeStruct((F, nodes), f32)),
            in_specs=[anywhere] * len(operands),
            out_specs=(vmem, vmem),
            scratch_shapes=[
                *(pltpu.VMEM(operand.shape, operand.dtype) for operand in operands),
                pltpu.SemaphoreType.DMA((len(operands),)),
                pltpu.VMEM((256, edges), bf16),
                pltpu.VMEM((256, edges), bf16),
                pltpu.VMEM((2, F, edges), f32),
                pltpu.VMEM((128, edges), bf16),
                pltpu.VMEM((LANES, LANES), i32),
                pltpu.VMEM((9, F, nodes), f32),
                pltpu.VMEM((2, 2 * F, LANES), bf16),
                pltpu.VMEM((12, F, LANES), bf16),
                pltpu.VMEM((3, F, 2 * LANES), bf16),
                pltpu.VMEM((4, len(FACES), 8, LANES), f32),
                pltpu.VMEM((4, 27, 1, LANES), f32),
                pltpu.VMEM((4, len(FACES), 8, LANES), f32),
                pltpu.VMEM((4, 27, 1, LANES), f32),
                pltpu.SemaphoreType.DMA((2,)),
                pltpu.SemaphoreType.DMA((4, 2)),
            ],
            compiler_params=pltpu.CompilerParams(collective_id=0, has_side_effects=True),
        )(*operands)

    split_columns = P(None, AXES)
    return jax.shard_map(
        on_device,
        mesh=mesh,
        in_specs=(split_columns, split_columns, split_columns, P(), P(), P(), P(), split_columns),
        out_specs=(split_columns, split_columns),
        check_vma=False,
    )
```

```python
import functools

import jax
import jax.numpy as jnp
from jax import lax
from jax.experimental import pallas as pl
from jax.experimental.pallas import tpu as pltpu
from jax.sharding import PartitionSpec as P

F = 32
LANES = 128
AXES = ("gx", "gy", "gz")
LINKS = [(k // 9 - 1, k // 3 % 3 - 1, k % 3 - 1) for k in range(27)]
REACH = [sum(abs(c) for c in offset) for offset in LINKS]
FACES = [k for k in range(27) if REACH[k] == 1]
RIMS = [k for k in range(27) if REACH[k] > 1]
ORDER = sorted(RIMS, key=lambda k: -REACH[k]) + FACES
RIM_ROW = 8 * len(FACES)
ROWS = 80
FORWARD_PRODUCTS = 16
BACKWARD_PRODUCTS = 8
f32, bf16, i32 = jnp.float32, jnp.bfloat16, jnp.int32


def split(value):
    high = value.astype(bf16)
    low = (value - high.astype(f32)).astype(bf16)
    return high, low


def dot(left, right):
    return lax.dot_general(left, right, (((1,), (0,)), ((), ())), preferred_element_type=f32)


def spread(matrix):
    rows = matrix.shape[0]
    wide = jnp.concatenate([matrix] * (LANES // matrix.shape[1]), axis=1)
    high, low = split(0.5 * wide)
    return jnp.where(iota((rows, LANES), 1) < LANES // 2, high.astype(f32), low.astype(f32)).astype(bf16)


def spread_flipped(matrix):
    rows = matrix.shape[0]
    tall = jnp.concatenate([matrix] * (LANES // rows), axis=0)
    wide = jnp.transpose(jnp.concatenate([tall, jnp.zeros((LANES, LANES - F), f32)], axis=1))[:F]
    high, low = split(0.5 * wide)
    if rows == 64:
        return jnp.concatenate([high, low], axis=1)
    return jnp.where(iota((F, LANES), 1) < LANES // 2, high.astype(f32), low.astype(f32)).astype(bf16)


def times(weights, value):
    high, low = split(value)
    return 2.0 * dot(weights, jnp.concatenate([high, low, high, low], axis=0))


def sigmoid_of(value):
    return 0.5 * jnp.tanh(0.5 * value) + 0.5


def lane_take(chunk, index):
    return jnp.take_along_axis(chunk, index, axis=1, mode="promise_in_bounds")


def iota(shape, dim):
    return lax.broadcasted_iota(i32, shape, dim)


def take(table, index):
    rows = table.shape[0]
    index = jnp.broadcast_to(index, (8, LANES))
    lane, part = index & (LANES - 1), index >> 7
    pieces = []
    for top in range(0, rows, 8):
        total = jnp.zeros((8, LANES), f32)
        for chunk in range(table.shape[1] // LANES):
            got = lane_take(table[top : top + 8, chunk * LANES : (chunk + 1) * LANES], lane)
            total = jnp.where(part == chunk, got, total)
        pieces.append(total)
    return jnp.concatenate(pieces, axis=0)


def kernel(
    sizes, x_hbm, edges_hbm, peers_hbm, edge_in_hbm, edge_out_hbm, node_in_hbm, node_out_hbm, cot_hbm,
    updated_ref, grad_ref,
    x_ref, edges_ref, peers_ref, edge_in_ref, edge_out_ref, node_in_ref, node_out_ref, cot_ref, load_sem,
    hot_target, hot_source, slopes, masked, peer_pad, held, ends_to, small_to, ends_from,
    face_out, rim_out, face_in, rim_in, send_sem, recv_sem,
):
    here = [lax.axis_index(axis) for axis in AXES]
    nodes = x_ref.shape[1]
    edges = edges_ref.shape[1]
    blocks = edges // LANES
    chunks = nodes // LANES

    def there(k):
        inside = None
        for place, step, size in zip(here, LINKS[k], sizes):
            if step:
                ok = place > 0 if step < 0 else place < size - 1
                inside = ok if inside is None else inside & ok
        return inside

    def device(k):
        return tuple(place + step for place, step in zip(here, LINKS[k]))

    def copy(turn, k):
        if REACH[k] == 1:
            source = face_out.at[turn, FACES.index(k)]
            target = face_in.at[turn, FACES.index(26 - k)]
        else:
            source = rim_out.at[turn, k]
            target = rim_in.at[turn, 26 - k]
        return pltpu.make_async_remote_copy(
            src_ref=source, dst_ref=target,
            send_sem=send_sem.at[min(REACH[k], 2) - 1], recv_sem=recv_sem.at[turn, min(REACH[k], 2) - 1],
            device_id=device(k), device_id_type=pl.DeviceIdType.MESH,
        )

    at_rim = jnp.int32(0)
    for place, size in zip(here, sizes):
        at_rim = at_rim + jnp.where((place == 0) | (place == size - 1), 1, 0).astype(i32)
    counts = [(6 - rim, 3 ** (3 - rim) * 2**rim - 7 + rim) for rim in range(4)]

    barrier = pltpu.get_barrier_semaphore()
    for k in ORDER:

        @pl.when(there(k))
        def _():
            pl.semaphore_signal(barrier, inc=1, device_id=device(k), device_id_type=pl.DeviceIdType.MESH)

    loads = [
        pltpu.make_async_copy(source, target, load_sem.at[at])
        for at, (source, target) in enumerate(
            (
                (x_hbm, x_ref), (edge_in_hbm, edge_in_ref), (edges_hbm, edges_ref), (peers_hbm, peers_ref),
                (edge_out_hbm, edge_out_ref), (node_in_hbm, node_in_ref), (node_out_hbm, node_out_ref),
                (cot_hbm, cot_ref),
            )
        )
    ]
    for load in loads:
        load.start()
    for load in loads:
        load.wait()

    def source_of(block):
        return edges_ref[0:1, block * LANES : (block + 1) * LANES]

    def target_of(block):
        return edges_ref[1:2, block * LANES : (block + 1) * LANES]

    def build_hot(hot, index_of):
        row = iota((256, LANES), 0)
        for block in range(blocks):
            index = jnp.broadcast_to(index_of(block) & 255, (256, LANES))
            hot[:, block * LANES : (block + 1) * LANES] = jnp.where(row == index, 1.0, 0.0).astype(bf16)

    peer_pad[...] = jnp.full(peer_pad.shape, 512, i32)
    peer_pad[0:27, 0 : peers_ref.shape[1]] = peers_ref[...]
    lane = iota((8, LANES), 1)
    group = iota((8, LANES), 0)
    by_slot = jnp.transpose(peer_pad[...].astype(f32)).astype(i32)[0:8]
    rim_index = lane - RIM_ROW
    slot_node = lane_take(by_slot, jnp.maximum(rim_index, 0))
    keep = jnp.zeros((8, LANES), jnp.bool_)
    for k in RIMS:
        keep = keep | (rim_index == k)
    slot_node = jnp.where(keep & (group < 4), slot_node, 512)
    for p, k in enumerate(FACES):
        row = jnp.broadcast_to(peer_pad[k : k + 1, :], (8, LANES))
        got = lane_take(row, 8 * group + (lane & 7))
        slot_node = jnp.where(lane >> 3 == p, got, slot_node)

    def node_slots():
        padded = jnp.concatenate([slot_node, jnp.full((LANES - 8, LANES), 512, i32)], axis=0)
        by_row = jnp.transpose(padded.astype(f32)).astype(i32)[0:ROWS]
        rows = iota((ROWS, LANES), 0)
        codes = []
        for chunk in range(chunks):
            node = iota((ROWS, LANES), 1) + chunk * LANES
            code = jnp.zeros((ROWS, LANES), f32)
            for g in range(4):
                column = jnp.broadcast_to(by_row[:, g : g + 1], (ROWS, LANES))
                code = code + jnp.where(column == node, rows + (LANES * g + 1), 0).astype(f32)
            codes.append(jnp.sum(code, axis=0, keepdims=True).astype(i32))
        return codes

    def pack(turn, field):
        columns = [take(field, slot_node[g : g + 1]) for g in range(4)]
        packed = jnp.transpose(jnp.concatenate(columns, axis=0))
        for p in range(len(FACES)):
            face_out[turn, p] = packed[8 * p : 8 * p + 8]
        for k in RIMS:
            rim_out[turn, k] = packed[RIM_ROW + k : RIM_ROW + k + 1]

    def send(turn):
        for k in ORDER:

            @pl.when(there(k))
            def _():
                copy(turn, k).start()

    def receive(turn):
        for rim, (faces, rims) in enumerate(counts):

            @pl.when(at_rim == rim)
            def _():
                landed = ((face_in.at[turn, 0:faces], 0), (rim_in.at[turn, 0:rims], 1))
                for block, which in landed:
                    pltpu.make_async_copy(block, block, recv_sem.at[turn, which]).wait()

    def unpack(turn, codes):
        faces = face_in[turn].reshape(RIM_ROW, LANES)
        rims = rim_in[turn].reshape(rim_in.shape[1], LANES)
        arrived = jnp.concatenate([faces, rims], axis=0)
        arrived = jnp.concatenate([arrived, jnp.zeros((LANES - arrived.shape[0], LANES), f32)], axis=0)
        columns = jnp.transpose(arrived)
        pieces = []
        for chunk in range(chunks):
            code = jnp.broadcast_to(codes[chunk] - 1, (8, LANES))
            row, which = code & (LANES - 1), code >> 7
            tops = []
            for top in range(0, F, 8):
                total = jnp.zeros((8, LANES), f32)
                for g in range(4):
                    got = lane_take(columns[F * g + top : F * g + top + 8], row)
                    total = jnp.where(which == g, got, total)
                tops.append(total)
            pieces.append(jnp.concatenate(tops, axis=0))
        return jnp.concatenate(pieces, axis=1)

    def put_masked(block, value, index):
        if 2 * block >= blocks:
            value = 0.5 * value
        half = jnp.broadcast_to(index >> 8, (F, LANES))
        columns = slice(block * LANES, (block + 1) * LANES)
        for part in range(2):
            high, low = split(jnp.where(half == part, value, 0.0))
            masked[64 * part : 64 * part + 32, columns] = high
            masked[64 * part + 32 : 64 * part + 64, columns] = low

    def scatter(hot):
        first, second = [
            lax.dot_general(
                masked[:, columns], hot[:, columns], (((1,), (1,)), ((), ())), preferred_element_type=f32
            )
            for columns in (slice(0, edges // 2), slice(edges // 2, edges))
        ]
        total = [first[at : at + 32] + 2.0 * second[at : at + 32] for at in range(0, 128, 32)]
        return jnp.concatenate([total[0] + total[1], total[2] + total[3]], axis=1)

    def take_target(table, start, stop):
        high, low = split(table)
        left = jnp.concatenate([high[:, :256], low[:, :256], high[:, 256:], low[:, 256:]], axis=0)
        pieces = []
        for block in range(start, stop, 2):
            width = min(2, stop - block)
            got = dot(left, hot_target[:, block * LANES : (block + width) * LANES])
            for at in range(width):
                half = jnp.broadcast_to(target_of(block + at) >> 8, (F, LANES))
                part = got[:, at * LANES : (at + 1) * LANES]
                lower = jnp.where(half == 0, part[0:32] + part[32:64], 0.0)
                pieces.append(jnp.where(half == 1, part[64:96] + part[96:128], lower))
        return pieces

    def by_target(table, products):
        return take_target(table, 0, products) + [take(table, target_of(block)) for block in range(products, blocks)]

    def edge_forward(layer, table):
        first, second = table[:F], table[F:]
        at_target = by_target(second, FORWARD_PRODUCTS)
        for block in range(blocks):
            pre = take(first, source_of(block)) + at_target[block]
            gate = sigmoid_of(pre)
            slopes[layer, :, block * LANES : (block + 1) * LANES] = gate * (1.0 + pre * (1.0 - gate))
            put_masked(block, pre * gate, target_of(block))
        return scatter(hot_target)

    def slope_sums(layer):
        for block in range(blocks):
            put_masked(block, slopes[layer, :, block * LANES : (block + 1) * LANES], target_of(block))
        return scatter(hot_target)

    def edge_backward(layer, table, summed):
        at_target = by_target(table, BACKWARD_PRODUCTS)
        for block in range(blocks):
            slope = slopes[layer, :, block * LANES : (block + 1) * LANES]
            put_masked(block, at_target[block] * slope, source_of(block))
        return jnp.concatenate([scatter(hot_source), table * summed], axis=0)

    def tiled(matrix):
        return jnp.concatenate([matrix] * 4, axis=1)

    own, out, mix, own_back, out_back, mix_back = [2 * at for at in range(6)]
    entry = [jnp.concatenate([edge_in_ref[layer][:, :F], edge_in_ref[layer][:, F:]], axis=0) for layer in range(2)]
    build_hot(hot_target, target_of)
    sums = edge_forward(0, times(spread(entry[0]), x_ref[...]))
    pack(0, sums)
    rim_counts = [f + r for f, r in counts]
    present = jnp.int32(rim_counts[0])
    for rim in range(1, 4):
        present = jnp.where(at_rim == rim, rim_counts[rim], present)
    pl.semaphore_wait(barrier, present)
    send(0)

    for layer in range(2):
        node = node_in_ref[layer]
        mixed = times(spread(node[:, F:]), tiled(edge_out_ref[layer]))[:, :F]
        small_to[own + layer] = spread(node[:, :F])
        small_to[out + layer] = spread(node_out_ref[layer])
        small_to[mix + layer] = spread(mixed)
        small_to[own_back + layer] = spread_flipped(node[:, :F])
        small_to[out_back + layer] = spread_flipped(node_out_ref[layer])
        small_to[mix_back + layer] = spread_flipped(mixed)
        ends_from[layer] = spread_flipped(entry[layer])
    ends_to[0] = spread(entry[1])
    through = times(ends_to[0], tiled(node_out_ref[0]))[:, :F]
    ends_to[1] = spread(through)
    ends_from[2] = spread_flipped(through)
    codes = node_slots()
    build_hot(hot_source, source_of)
    held[4] = slope_sums(0)
    field = x_ref[...]
    held[0] = times(small_to[own], field)
    both_ends = times(ends_to[0], field)
    held[5] = both_ends[:F]
    held[6] = both_ends[F:]
    receive(0)
    pre = held[0] + times(small_to[mix], sums + unpack(0, codes))
    gate = sigmoid_of(pre)
    active = pre * gate
    held[7] = gate * (1.0 + pre * (1.0 - gate))
    table = jnp.concatenate([held[5], held[6]], axis=0) + times(ends_to[1], active)
    sums = edge_forward(1, table)
    pack(1, sums)
    send(1)
    field = field + times(small_to[out], active)
    held[1] = times(small_to[own + 1], field)
    held[8] = times(small_to[out_back + 1], cot_ref[...])
    held[5] = slope_sums(1)
    receive(1)
    pre = held[1] + times(small_to[mix + 1], sums + unpack(1, codes))
    gate = sigmoid_of(pre)

    delta = held[8] * (gate * (1.0 + pre * (1.0 - gate)))
    sums = times(small_to[mix_back + 1], delta)
    pack(2, sums)
    send(2)
    updated_ref[...] = field + times(small_to[out + 1], pre * gate)
    held[2] = cot_ref[...] + times(small_to[own_back + 1], delta)
    held[6] = times(small_to[out_back], held[2])
    receive(2)
    both = edge_backward(1, sums + unpack(2, codes), held[5])
    delta = (held[6] + times(ends_from[2], both)) * held[7]
    sums = times(small_to[mix_back], delta)
    pack(3, sums)
    send(3)
    held[3] = held[2] + times(ends_from[1], both) + times(small_to[own_back], delta)
    receive(3)
    both = edge_backward(0, sums + unpack(3, codes), held[4])
    grad_ref[...] = held[3] + times(ends_from[0], both)

    for rim, (faces, rims) in enumerate(counts):

        @pl.when(at_rim == rim)
        def _():
            for block, which in ((face_out.at[:, 0:faces], 0), (rim_out.at[:, 0:rims], 1)):
                pltpu.make_async_copy(block, block, send_sem.at[which]).wait()


def solution(mesh):
    sizes = tuple(mesh.shape[axis] for axis in AXES)

    def on_device(*operands):
        nodes = operands[0].shape[1]
        edges = operands[1].shape[1]
        anywhere = pl.BlockSpec(memory_space=pl.ANY)
        vmem = pl.BlockSpec(memory_space=pltpu.VMEM)
        return pl.pallas_call(
            functools.partial(kernel, sizes),
            out_shape=(pltpu.VMEM((F, nodes), f32), pltpu.VMEM((F, nodes), f32)),
            in_specs=[anywhere] * len(operands),
            out_specs=(vmem, vmem),
            scratch_shapes=[
                *(pltpu.VMEM(operand.shape, operand.dtype) for operand in operands),
                pltpu.SemaphoreType.DMA((len(operands),)),
                pltpu.VMEM((256, edges), bf16),
                pltpu.VMEM((256, edges), bf16),
                pltpu.VMEM((2, F, edges), f32),
                pltpu.VMEM((128, edges), bf16),
                pltpu.VMEM((LANES, LANES), i32),
                pltpu.VMEM((9, F, nodes), f32),
                pltpu.VMEM((2, 2 * F, LANES), bf16),
                pltpu.VMEM((12, F, LANES), bf16),
                pltpu.VMEM((3, F, 2 * LANES), bf16),
                pltpu.VMEM((4, len(FACES), 8, LANES), f32),
                pltpu.VMEM((4, 27, 1, LANES), f32),
                pltpu.VMEM((4, len(FACES), 8, LANES), f32),
                pltpu.VMEM((4, 27, 1, LANES), f32),
                pltpu.SemaphoreType.DMA((2,)),
                pltpu.SemaphoreType.DMA((4, 2)),
            ],
            compiler_params=pltpu.CompilerParams(collective_id=0, has_side_effects=True),
        )(*operands)

    split_columns = P(None, AXES)
    return jax.shard_map(
        on_device,
        mesh=mesh,
        in_specs=(split_columns, split_columns, split_columns, P(), P(), P(), P(), split_columns),
        out_specs=(split_columns, split_columns),
        check_vma=False,
    )
```

```python
import functools

import jax
import jax.numpy as jnp
from jax import lax
from jax.experimental import pallas as pl
from jax.experimental.pallas import tpu as pltpu
from jax.sharding import PartitionSpec as P

F = 32
LANES = 128
AXES = ("gx", "gy", "gz")
LINKS = [(k // 9 - 1, k // 3 % 3 - 1, k % 3 - 1) for k in range(27)]
REACH = [sum(abs(c) for c in offset) for offset in LINKS]
FACES = [k for k in range(27) if REACH[k] == 1]
RIMS = [k for k in range(27) if REACH[k] > 1]
ORDER = sorted(RIMS, key=lambda k: -REACH[k]) + FACES
RIM_ROW = 8 * len(FACES)
ROWS = 80
SOURCE_PRODUCTS = 6
FORWARD_PRODUCTS = 16
BACKWARD_PRODUCTS = 8
f32, bf16, i32 = jnp.float32, jnp.bfloat16, jnp.int32


def split(value):
    high = value.astype(bf16)
    low = (value - high.astype(f32)).astype(bf16)
    return high, low


def dot(left, right):
    return lax.dot_general(left, right, (((1,), (0,)), ((), ())), preferred_element_type=f32)


def spread(matrix):
    rows = matrix.shape[0]
    wide = jnp.concatenate([matrix] * (LANES // matrix.shape[1]), axis=1)
    high, low = split(0.5 * wide)
    return jnp.where(iota((rows, LANES), 1) < LANES // 2, high.astype(f32), low.astype(f32)).astype(bf16)


def spread_flipped(matrix):
    rows = matrix.shape[0]
    tall = jnp.concatenate([matrix] * (LANES // rows), axis=0)
    wide = jnp.transpose(jnp.concatenate([tall, jnp.zeros((LANES, LANES - F), f32)], axis=1))[:F]
    high, low = split(0.5 * wide)
    if rows == 64:
        return jnp.concatenate([high, low], axis=1)
    return jnp.where(iota((F, LANES), 1) < LANES // 2, high.astype(f32), low.astype(f32)).astype(bf16)


def times(weights, value):
    high, low = split(value)
    return 2.0 * dot(weights, jnp.concatenate([high, low, high, low], axis=0))


def sigmoid_of(value):
    return 0.5 * jnp.tanh(0.5 * value) + 0.5


def lane_take(chunk, index):
    return jnp.take_along_axis(chunk, index, axis=1, mode="promise_in_bounds")


def iota(shape, dim):
    return lax.broadcasted_iota(i32, shape, dim)


def take(table, index):
    rows = table.shape[0]
    index = jnp.broadcast_to(index, (8, LANES))
    lane, part = index & (LANES - 1), index >> 7
    pieces = []
    for top in range(0, rows, 8):
        total = jnp.zeros((8, LANES), f32)
        for chunk in range(table.shape[1] // LANES):
            got = lane_take(table[top : top + 8, chunk * LANES : (chunk + 1) * LANES], lane)
            total = jnp.where(part == chunk, got, total)
        pieces.append(total)
    return jnp.concatenate(pieces, axis=0)


def kernel(
    sizes, x_hbm, edges_hbm, peers_hbm, edge_in_hbm, edge_out_hbm, node_in_hbm, node_out_hbm, cot_hbm,
    updated_ref, grad_ref,
    x_ref, edges_ref, peers_ref, edge_in_ref, edge_out_ref, node_in_ref, node_out_ref, cot_ref, load_sem,
    hot_target, hot_source, slopes, masked, peer_pad, held, ends_to, small_to, ends_from,
    face_out, rim_out, face_in, rim_in, send_sem, recv_sem,
):
    here = [lax.axis_index(axis) for axis in AXES]
    nodes = x_ref.shape[1]
    edges = edges_ref.shape[1]
    blocks = edges // LANES
    chunks = nodes // LANES

    def there(k):
        inside = None
        for place, step, size in zip(here, LINKS[k], sizes):
            if step:
                ok = place > 0 if step < 0 else place < size - 1
                inside = ok if inside is None else inside & ok
        return inside

    def device(k):
        return tuple(place + step for place, step in zip(here, LINKS[k]))

    def copy(turn, k):
        if REACH[k] == 1:
            source = face_out.at[turn, FACES.index(k)]
            target = face_in.at[turn, FACES.index(26 - k)]
        else:
            source = rim_out.at[turn, k]
            target = rim_in.at[turn, 26 - k]
        return pltpu.make_async_remote_copy(
            src_ref=source, dst_ref=target,
            send_sem=send_sem.at[min(REACH[k], 2) - 1], recv_sem=recv_sem.at[turn, min(REACH[k], 2) - 1],
            device_id=device(k), device_id_type=pl.DeviceIdType.MESH,
        )

    at_rim = jnp.int32(0)
    for place, size in zip(here, sizes):
        at_rim = at_rim + jnp.where((place == 0) | (place == size - 1), 1, 0).astype(i32)
    counts = [(6 - rim, 3 ** (3 - rim) * 2**rim - 7 + rim) for rim in range(4)]

    barrier = pltpu.get_barrier_semaphore()
    for k in ORDER:

        @pl.when(there(k))
        def _():
            pl.semaphore_signal(barrier, inc=1, device_id=device(k), device_id_type=pl.DeviceIdType.MESH)

    loads = [
        pltpu.make_async_copy(source, target, load_sem.at[at])
        for at, (source, target) in enumerate(
            (
                (x_hbm, x_ref), (edge_in_hbm, edge_in_ref), (edges_hbm, edges_ref), (peers_hbm, peers_ref),
                (edge_out_hbm, edge_out_ref), (node_in_hbm, node_in_ref), (node_out_hbm, node_out_ref),
                (cot_hbm, cot_ref),
            )
        )
    ]
    for load in loads:
        load.start()
    for load in loads:
        load.wait()

    def source_of(block):
        return edges_ref[0:1, block * LANES : (block + 1) * LANES]

    def target_of(block):
        return edges_ref[1:2, block * LANES : (block + 1) * LANES]

    def build_hot(hot, index_of):
        row = iota((256, LANES), 0)
        for block in range(blocks):
            index = jnp.broadcast_to(index_of(block) & 255, (256, LANES))
            hot[:, block * LANES : (block + 1) * LANES] = jnp.where(row == index, 1.0, 0.0).astype(bf16)

    peer_pad[...] = jnp.full(peer_pad.shape, 512, i32)
    peer_pad[0:27, 0 : peers_ref.shape[1]] = peers_ref[...]
    lane = iota((8, LANES), 1)
    group = iota((8, LANES), 0)
    by_slot = jnp.transpose(peer_pad[...].astype(f32)).astype(i32)[0:8]
    rim_index = lane - RIM_ROW
    slot_node = lane_take(by_slot, jnp.maximum(rim_index, 0))
    keep = jnp.zeros((8, LANES), jnp.bool_)
    for k in RIMS:
        keep = keep | (rim_index == k)
    slot_node = jnp.where(keep & (group < 4), slot_node, 512)
    for p, k in enumerate(FACES):
        row = jnp.broadcast_to(peer_pad[k : k + 1, :], (8, LANES))
        got = lane_take(row, 8 * group + (lane & 7))
        slot_node = jnp.where(lane >> 3 == p, got, slot_node)

    def node_slots():
        padded = jnp.concatenate([slot_node, jnp.full((LANES - 8, LANES), 512, i32)], axis=0)
        by_row = jnp.transpose(padded.astype(f32)).astype(i32)[0:ROWS]
        rows = iota((ROWS, LANES), 0)
        codes = []
        for chunk in range(chunks):
            node = iota((ROWS, LANES), 1) + chunk * LANES
            code = jnp.zeros((ROWS, LANES), f32)
            for g in range(4):
                column = jnp.broadcast_to(by_row[:, g : g + 1], (ROWS, LANES))
                code = code + jnp.where(column == node, rows + (LANES * g + 1), 0).astype(f32)
            codes.append(jnp.sum(code, axis=0, keepdims=True).astype(i32))
        return codes

    def at_slots(field):
        return jnp.concatenate([take(field, slot_node[g : g + 1]) for g in range(4)], axis=1)

    def ship(turn, columns):
        tall = jnp.concatenate([columns[:, g * LANES : (g + 1) * LANES] for g in range(4)], axis=0)
        packed = jnp.transpose(tall)
        for p in range(len(FACES)):
            face_out[turn, p] = packed[8 * p : 8 * p + 8]
        for k in RIMS:
            rim_out[turn, k] = packed[RIM_ROW + k : RIM_ROW + k + 1]

    def send(turn):
        for k in ORDER:

            @pl.when(there(k))
            def _():
                copy(turn, k).start()

    def receive(turn):
        for rim, (faces, rims) in enumerate(counts):

            @pl.when(at_rim == rim)
            def _():
                landed = ((face_in.at[turn, 0:faces], 0), (rim_in.at[turn, 0:rims], 1))
                for block, which in landed:
                    pltpu.make_async_copy(block, block, recv_sem.at[turn, which]).wait()

    def arrivals(turn):
        faces = face_in[turn].reshape(RIM_ROW, LANES)
        rims = rim_in[turn].reshape(rim_in.shape[1], LANES)
        arrived = jnp.concatenate([faces, rims], axis=0)
        arrived = jnp.concatenate([arrived, jnp.zeros((LANES - arrived.shape[0], LANES), f32)], axis=0)
        return jnp.transpose(arrived)

    def unpack(turn, codes):
        columns = arrivals(turn)
        pieces = []
        for chunk in range(chunks):
            code = jnp.broadcast_to(codes[chunk] - 1, (8, LANES))
            row, which = code & (LANES - 1), code >> 7
            tops = []
            for top in range(0, F, 8):
                total = jnp.zeros((8, LANES), f32)
                for g in range(4):
                    got = lane_take(columns[F * g + top : F * g + top + 8], row)
                    total = jnp.where(which == g, got, total)
                tops.append(total)
            pieces.append(jnp.concatenate(tops, axis=0))
        return jnp.concatenate(pieces, axis=1)

    def put_masked(block, value, index):
        if 2 * block >= blocks:
            value = 0.5 * value
        half = jnp.broadcast_to(index >> 8, (F, LANES))
        columns = slice(block * LANES, (block + 1) * LANES)
        for part in range(2):
            high, low = split(jnp.where(half == part, value, 0.0))
            masked[64 * part : 64 * part + 32, columns] = high
            masked[64 * part + 32 : 64 * part + 64, columns] = low

    def scatter(hot):
        first, second = [
            lax.dot_general(
                masked[:, columns], hot[:, columns], (((1,), (1,)), ((), ())), preferred_element_type=f32
            )
            for columns in (slice(0, edges // 2), slice(edges // 2, edges))
        ]
        total = [first[at : at + 32] + 2.0 * second[at : at + 32] for at in range(0, 128, 32)]
        return jnp.concatenate([total[0] + total[1], total[2] + total[3]], axis=1)

    def take_products(table, hot, index_of, stop):
        high, low = split(table)
        left = jnp.concatenate([high[:, :256], low[:, :256], high[:, 256:], low[:, 256:]], axis=0)
        pieces = []
        for block in range(0, stop, 2):
            got = dot(left, hot[:, block * LANES : (block + 2) * LANES])
            for at in range(2):
                half = jnp.broadcast_to(index_of(block + at) >> 8, (F, LANES))
                part = got[:, at * LANES : (at + 1) * LANES]
                lower = jnp.where(half == 0, part[0:32] + part[32:64], 0.0)
                pieces.append(jnp.where(half == 1, part[64:96] + part[96:128], lower))
        return pieces

    def at_ends(table, hot, index_of, products):
        pieces = take_products(table, hot, index_of, products)
        return pieces + [take(table, index_of(block)) for block in range(products, blocks)]

    def edge_forward(layer, table):
        first, second = table[:F], table[F:]
        at_target = at_ends(second, hot_target, target_of, FORWARD_PRODUCTS)
        at_source = at_ends(first, hot_source, source_of, SOURCE_PRODUCTS if layer else 0)
        for block in range(blocks):
            pre = at_source[block] + at_target[block]
            gate = sigmoid_of(pre)
            slopes[layer, :, block * LANES : (block + 1) * LANES] = gate * (1.0 + pre * (1.0 - gate))
            put_masked(block, pre * gate, target_of(block))
        return scatter(hot_target)

    def slope_sums(layer):
        for block in range(blocks):
            put_masked(block, slopes[layer, :, block * LANES : (block + 1) * LANES], target_of(block))
        return scatter(hot_target)

    def edge_backward(layer, table, summed):
        at_target = at_ends(table, hot_target, target_of, BACKWARD_PRODUCTS)
        for block in range(blocks):
            slope = slopes[layer, :, block * LANES : (block + 1) * LANES]
            put_masked(block, at_target[block] * slope, source_of(block))
        return jnp.concatenate([scatter(hot_source), table * summed], axis=0)

    def tiled(matrix):
        return jnp.concatenate([matrix] * 4, axis=1)

    own, out, mix, own_back, out_back, mix_back = [2 * at for at in range(6)]
    entry = [jnp.concatenate([edge_in_ref[layer][:, :F], edge_in_ref[layer][:, F:]], axis=0) for layer in range(2)]
    build_hot(hot_target, target_of)
    sums = edge_forward(0, times(spread(entry[0]), x_ref[...]))
    ship(0, at_slots(sums))
    rim_counts = [f + r for f, r in counts]
    present = jnp.int32(rim_counts[0])
    for rim in range(1, 4):
        present = jnp.where(at_rim == rim, rim_counts[rim], present)
    pl.semaphore_wait(barrier, present)
    send(0)

    for layer in range(2):
        node = node_in_ref[layer]
        mixed = times(spread(node[:, F:]), tiled(edge_out_ref[layer]))[:, :F]
        small_to[own + layer] = spread(node[:, :F])
        small_to[out + layer] = spread(node_out_ref[layer])
        small_to[mix + layer] = spread(mixed)
        small_to[own_back + layer] = spread_flipped(node[:, :F])
        small_to[out_back + layer] = spread_flipped(node_out_ref[layer])
        small_to[mix_back + layer] = spread_flipped(mixed)
        ends_from[layer] = spread_flipped(entry[layer])
    ends_to[0] = spread(entry[1])
    through = times(ends_to[0], tiled(node_out_ref[0]))[:, :F]
    ends_to[1] = spread(through)
    ends_from[2] = spread_flipped(through)
    codes = node_slots()
    build_hot(hot_source, source_of)
    held[4] = slope_sums(0)
    field = x_ref[...]
    held[0] = times(small_to[own], field)
    both_ends = times(ends_to[0], field)
    held[5] = both_ends[:F]
    held[6] = both_ends[F:]
    receive(0)
    pre = held[0] + times(small_to[mix], sums + unpack(0, codes))
    gate = sigmoid_of(pre)
    active = pre * gate
    held[7] = gate * (1.0 + pre * (1.0 - gate))
    table = jnp.concatenate([held[5], held[6]], axis=0) + times(ends_to[1], active)
    sums = edge_forward(1, table)
    ship(1, at_slots(sums))
    send(1)
    field = field + times(small_to[out], active)
    held[1] = times(small_to[own + 1], field)
    held[8] = times(small_to[out_back + 1], cot_ref[...])
    held[5] = slope_sums(1)
    local = held[1] + times(small_to[mix + 1], sums)
    held[9] = at_slots(local)
    held[10] = at_slots(held[8])
    receive(1)
    arrived = arrivals(1)
    arrived = jnp.concatenate([arrived[F * g : F * g + F] for g in range(4)], axis=1)
    pre = held[9] + times(small_to[mix + 1], arrived)
    gate = sigmoid_of(pre)
    delta = held[10] * (gate * (1.0 + pre * (1.0 - gate)))
    ship(2, times(small_to[mix_back + 1], delta))
    send(2)
    pre = held[1] + times(small_to[mix + 1], sums + unpack(1, codes))
    gate = sigmoid_of(pre)
    delta = held[8] * (gate * (1.0 + pre * (1.0 - gate)))
    sums = times(small_to[mix_back + 1], delta)
    updated_ref[...] = field + times(small_to[out + 1], pre * gate)
    held[2] = cot_ref[...] + times(small_to[own_back + 1], delta)
    held[6] = times(small_to[out_back], held[2])
    receive(2)
    both = edge_backward(1, sums + unpack(2, codes), held[5])
    delta = (held[6] + times(ends_from[2], both)) * held[7]
    sums = times(small_to[mix_back], delta)
    ship(3, at_slots(sums))
    send(3)
    held[3] = held[2] + times(ends_from[1], both) + times(small_to[own_back], delta)
    receive(3)
    both = edge_backward(0, sums + unpack(3, codes), held[4])
    grad_ref[...] = held[3] + times(ends_from[0], both)

    for rim, (faces, rims) in enumerate(counts):

        @pl.when(at_rim == rim)
        def _():
            for block, which in ((face_out.at[:, 0:faces], 0), (rim_out.at[:, 0:rims], 1)):
                pltpu.make_async_copy(block, block, send_sem.at[which]).wait()


def solution(mesh):
    sizes = tuple(mesh.shape[axis] for axis in AXES)

    def on_device(*operands):
        nodes = operands[0].shape[1]
        edges = operands[1].shape[1]
        anywhere = pl.BlockSpec(memory_space=pl.ANY)
        vmem = pl.BlockSpec(memory_space=pltpu.VMEM)
        return pl.pallas_call(
            functools.partial(kernel, sizes),
            out_shape=(pltpu.VMEM((F, nodes), f32), pltpu.VMEM((F, nodes), f32)),
            in_specs=[anywhere] * len(operands),
            out_specs=(vmem, vmem),
            scratch_shapes=[
                *(pltpu.VMEM(operand.shape, operand.dtype) for operand in operands),
                pltpu.SemaphoreType.DMA((len(operands),)),
                pltpu.VMEM((256, edges), bf16),
                pltpu.VMEM((256, edges), bf16),
                pltpu.VMEM((2, F, edges), f32),
                pltpu.VMEM((128, edges), bf16),
                pltpu.VMEM((LANES, LANES), i32),
                pltpu.VMEM((11, F, nodes), f32),
                pltpu.VMEM((2, 2 * F, LANES), bf16),
                pltpu.VMEM((12, F, LANES), bf16),
                pltpu.VMEM((3, F, 2 * LANES), bf16),
                pltpu.VMEM((4, len(FACES), 8, LANES), f32),
                pltpu.VMEM((4, 27, 1, LANES), f32),
                pltpu.VMEM((4, len(FACES), 8, LANES), f32),
                pltpu.VMEM((4, 27, 1, LANES), f32),
                pltpu.SemaphoreType.DMA((2,)),
                pltpu.SemaphoreType.DMA((4, 2)),
            ],
            compiler_params=pltpu.CompilerParams(collective_id=0, has_side_effects=True),
        )(*operands)

    split_columns = P(None, AXES)
    return jax.shard_map(
        on_device,
        mesh=mesh,
        in_specs=(split_columns, split_columns, split_columns, P(), P(), P(), P(), split_columns),
        out_specs=(split_columns, split_columns),
        check_vma=False,
    )
```

```python
import functools

import jax
import jax.numpy as jnp
from jax import lax
from jax.experimental import pallas as pl
from jax.experimental.pallas import tpu as pltpu
from jax.sharding import PartitionSpec as P

F = 32
LANES = 128
AXES = ("gx", "gy", "gz")
LINKS = [(k // 9 - 1, k // 3 % 3 - 1, k % 3 - 1) for k in range(27)]
REACH = [sum(abs(c) for c in offset) for offset in LINKS]
FACES = [k for k in range(27) if REACH[k] == 1]
RIMS = [k for k in range(27) if REACH[k] > 1]
ORDER = sorted(RIMS, key=lambda k: -REACH[k]) + FACES
RIM_ROW = 8 * len(FACES)
ROWS = 80
SOURCE_PRODUCTS = 6
FORWARD_PRODUCTS = 16
BACKWARD_PRODUCTS = 8
f32, bf16, i32 = jnp.float32, jnp.bfloat16, jnp.int32


def split(value):
    high = value.astype(bf16)
    low = (value - high.astype(f32)).astype(bf16)
    return high, low


def dot(left, right):
    return lax.dot_general(left, right, (((1,), (0,)), ((), ())), preferred_element_type=f32)


def spread(matrix):
    rows = matrix.shape[0]
    wide = jnp.concatenate([matrix] * (LANES // matrix.shape[1]), axis=1)
    high, low = split(0.5 * wide)
    return jnp.where(iota((rows, LANES), 1) < LANES // 2, high.astype(f32), low.astype(f32)).astype(bf16)


def spread_flipped(matrix):
    rows = matrix.shape[0]
    tall = jnp.concatenate([matrix] * (LANES // rows), axis=0)
    wide = jnp.transpose(jnp.concatenate([tall, jnp.zeros((LANES, LANES - F), f32)], axis=1))[:F]
    high, low = split(0.5 * wide)
    if rows == 64:
        return jnp.concatenate([high, low], axis=1)
    return jnp.where(iota((F, LANES), 1) < LANES // 2, high.astype(f32), low.astype(f32)).astype(bf16)


def times(weights, value):
    high, low = split(value)
    return 2.0 * dot(weights, jnp.concatenate([high, low, high, low], axis=0))


def sigmoid_of(value):
    return 0.5 * jnp.tanh(0.5 * value) + 0.5


def lane_take(chunk, index):
    return jnp.take_along_axis(chunk, index, axis=1, mode="promise_in_bounds")


def iota(shape, dim):
    return lax.broadcasted_iota(i32, shape, dim)


def take(table, index):
    rows = table.shape[0]
    index = jnp.broadcast_to(index, (8, LANES))
    lane, part = index & (LANES - 1), index >> 7
    pieces = []
    for top in range(0, rows, 8):
        total = jnp.zeros((8, LANES), f32)
        for chunk in range(table.shape[1] // LANES):
            got = lane_take(table[top : top + 8, chunk * LANES : (chunk + 1) * LANES], lane)
            total = jnp.where(part == chunk, got, total)
        pieces.append(total)
    return jnp.concatenate(pieces, axis=0)


def kernel(
    sizes, x_hbm, edges_hbm, peers_hbm, edge_in_hbm, edge_out_hbm, node_in_hbm, node_out_hbm, cot_hbm,
    updated_ref, grad_ref,
    x_ref, edges_ref, peers_ref, edge_in_ref, edge_out_ref, node_in_ref, node_out_ref, cot_ref, load_sem,
    hot_target, hot_source, slopes, masked, peer_pad, held, ends_to, small_to, ends_from,
    face_out, rim_out, face_in, rim_in, send_sem, recv_sem,
):
    here = [lax.axis_index(axis) for axis in AXES]
    nodes = x_ref.shape[1]
    edges = edges_ref.shape[1]
    blocks = edges // LANES
    chunks = nodes // LANES

    def there(k):
        inside = None
        for place, step, size in zip(here, LINKS[k], sizes):
            if step:
                ok = place > 0 if step < 0 else place < size - 1
                inside = ok if inside is None else inside & ok
        return inside

    def device(k):
        return tuple(place + step for place, step in zip(here, LINKS[k]))

    def copy(turn, k):
        if REACH[k] == 1:
            source = face_out.at[turn, FACES.index(k)]
            target = face_in.at[turn, FACES.index(26 - k)]
        else:
            source = rim_out.at[turn, k]
            target = rim_in.at[turn, 26 - k]
        return pltpu.make_async_remote_copy(
            src_ref=source, dst_ref=target,
            send_sem=send_sem.at[min(REACH[k], 2) - 1], recv_sem=recv_sem.at[turn, min(REACH[k], 2) - 1],
            device_id=device(k), device_id_type=pl.DeviceIdType.MESH,
        )

    at_rim = jnp.int32(0)
    for place, size in zip(here, sizes):
        at_rim = at_rim + jnp.where((place == 0) | (place == size - 1), 1, 0).astype(i32)
    counts = [(6 - rim, 3 ** (3 - rim) * 2**rim - 7 + rim) for rim in range(4)]

    barrier = pltpu.get_barrier_semaphore()
    for k in ORDER:

        @pl.when(there(k))
        def _():
            pl.semaphore_signal(barrier, inc=1, device_id=device(k), device_id_type=pl.DeviceIdType.MESH)

    loads = [
        pltpu.make_async_copy(source, target, load_sem.at[at])
        for at, (source, target) in enumerate(
            (
                (x_hbm, x_ref), (edge_in_hbm, edge_in_ref), (edges_hbm, edges_ref), (peers_hbm, peers_ref),
                (edge_out_hbm, edge_out_ref), (node_in_hbm, node_in_ref), (node_out_hbm, node_out_ref),
                (cot_hbm, cot_ref),
            )
        )
    ]
    for load in loads:
        load.start()
    for load in loads:
        load.wait()

    def source_of(block):
        return edges_ref[0:1, block * LANES : (block + 1) * LANES]

    def target_of(block):
        return edges_ref[1:2, block * LANES : (block + 1) * LANES]

    def build_hot(hot, index_of):
        row = iota((256, LANES), 0)
        for block in range(blocks):
            index = jnp.broadcast_to(index_of(block) & 255, (256, LANES))
            hot[:, block * LANES : (block + 1) * LANES] = jnp.where(row == index, 1.0, 0.0).astype(bf16)

    peer_pad[...] = jnp.full(peer_pad.shape, 512, i32)
    peer_pad[0:27, 0 : peers_ref.shape[1]] = peers_ref[...]
    lane = iota((8, LANES), 1)
    group = iota((8, LANES), 0)
    by_slot = jnp.transpose(peer_pad[...].astype(f32)).astype(i32)[0:8]
    rim_index = lane - RIM_ROW
    slot_node = lane_take(by_slot, jnp.maximum(rim_index, 0))
    keep = jnp.zeros((8, LANES), jnp.bool_)
    for k in RIMS:
        keep = keep | (rim_index == k)
    slot_node = jnp.where(keep & (group < 4), slot_node, 512)
    for p, k in enumerate(FACES):
        row = jnp.broadcast_to(peer_pad[k : k + 1, :], (8, LANES))
        got = lane_take(row, 8 * group + (lane & 7))
        slot_node = jnp.where(lane >> 3 == p, got, slot_node)

    def node_slots():
        padded = jnp.concatenate([slot_node, jnp.full((LANES - 8, LANES), 512, i32)], axis=0)
        by_row = jnp.transpose(padded.astype(f32)).astype(i32)[0:ROWS]
        rows = iota((ROWS, LANES), 0)
        codes = []
        for chunk in range(chunks):
            node = iota((ROWS, LANES), 1) + chunk * LANES
            code = jnp.zeros((ROWS, LANES), f32)
            for g in range(4):
                column = jnp.broadcast_to(by_row[:, g : g + 1], (ROWS, LANES))
                code = code + jnp.where(column == node, rows + (LANES * g + 1), 0).astype(f32)
            codes.append(jnp.sum(code, axis=0, keepdims=True).astype(i32))
        return codes

    def at_slots(field):
        return jnp.concatenate([take(field, slot_node[g : g + 1]) for g in range(4)], axis=1)

    def ship(turn, columns):
        tall = jnp.concatenate([columns[:, g * LANES : (g + 1) * LANES] for g in range(4)], axis=0)
        packed = jnp.transpose(tall)
        for p in range(len(FACES)):
            face_out[turn, p] = packed[8 * p : 8 * p + 8]
        for k in RIMS:
            rim_out[turn, k] = packed[RIM_ROW + k : RIM_ROW + k + 1]

    def send(turn):
        for k in ORDER:

            @pl.when(there(k))
            def _():
                copy(turn, k).start()

    def receive(turn):
        for rim, (faces, rims) in enumerate(counts):

            @pl.when(at_rim == rim)
            def _():
                landed = ((face_in.at[turn, 0:faces], 0), (rim_in.at[turn, 0:rims], 1))
                for block, which in landed:
                    pltpu.make_async_copy(block, block, recv_sem.at[turn, which]).wait()

    def arrivals(turn):
        faces = face_in[turn].reshape(RIM_ROW, LANES)
        rims = rim_in[turn].reshape(rim_in.shape[1], LANES)
        arrived = jnp.concatenate([faces, rims], axis=0)
        arrived = jnp.concatenate([arrived, jnp.zeros((LANES - arrived.shape[0], LANES), f32)], axis=0)
        return jnp.transpose(arrived)

    def unpack(turn, codes):
        columns = arrivals(turn)
        pieces = []
        for chunk in range(chunks):
            code = jnp.broadcast_to(codes[chunk] - 1, (8, LANES))
            row, which = code & (LANES - 1), code >> 7
            tops = []
            for top in range(0, F, 8):
                total = jnp.zeros((8, LANES), f32)
                for g in range(4):
                    got = lane_take(columns[F * g + top : F * g + top + 8], row)
                    total = jnp.where(which == g, got, total)
                tops.append(total)
            pieces.append(jnp.concatenate(tops, axis=0))
        return jnp.concatenate(pieces, axis=1)

    def put_masked(block, value, index):
        if 2 * block >= blocks:
            value = 0.5 * value
        half = jnp.broadcast_to(index >> 8, (F, LANES))
        columns = slice(block * LANES, (block + 1) * LANES)
        for part in range(2):
            high, low = split(jnp.where(half == part, value, 0.0))
            masked[64 * part : 64 * part + 32, columns] = high
            masked[64 * part + 32 : 64 * part + 64, columns] = low

    def scatter(hot):
        first, second = [
            lax.dot_general(
                masked[:, columns], hot[:, columns], (((1,), (1,)), ((), ())), preferred_element_type=f32
            )
            for columns in (slice(0, edges // 2), slice(edges // 2, edges))
        ]
        total = [first[at : at + 32] + 2.0 * second[at : at + 32] for at in range(0, 128, 32)]
        return jnp.concatenate([total[0] + total[1], total[2] + total[3]], axis=1)

    def take_products(table, hot, index_of, stop):
        high, low = split(table)
        left = jnp.concatenate([high[:, :256], low[:, :256], high[:, 256:], low[:, 256:]], axis=0)
        pieces = []
        for block in range(0, stop, 2):
            got = dot(left, hot[:, block * LANES : (block + 2) * LANES])
            for at in range(2):
                half = jnp.broadcast_to(index_of(block + at) >> 8, (F, LANES))
                part = got[:, at * LANES : (at + 1) * LANES]
                lower = jnp.where(half == 0, part[0:32] + part[32:64], 0.0)
                pieces.append(jnp.where(half == 1, part[64:96] + part[96:128], lower))
        return pieces

    def at_ends(table, hot, index_of, products):
        pieces = take_products(table, hot, index_of, products)
        return pieces + [take(table, index_of(block)) for block in range(products, blocks)]

    def edge_forward(layer, table):
        first, second = table[:F], table[F:]
        at_target = at_ends(second, hot_target, target_of, FORWARD_PRODUCTS)
        at_source = at_ends(first, hot_source, source_of, SOURCE_PRODUCTS if layer else 0)
        for block in range(blocks):
            pre = at_source[block] + at_target[block]
            gate = sigmoid_of(pre)
            slopes[layer, :, block * LANES : (block + 1) * LANES] = gate * (1.0 + pre * (1.0 - gate))
            put_masked(block, pre * gate, target_of(block))
        return scatter(hot_target)

    def slope_sums(layer):
        for block in range(blocks):
            put_masked(block, slopes[layer, :, block * LANES : (block + 1) * LANES], target_of(block))
        return scatter(hot_target)

    def edge_backward(layer, table, summed):
        at_target = at_ends(table, hot_target, target_of, BACKWARD_PRODUCTS)
        for block in range(blocks):
            slope = slopes[layer, :, block * LANES : (block + 1) * LANES]
            put_masked(block, at_target[block] * slope, source_of(block))
        return jnp.concatenate([scatter(hot_source), table * summed], axis=0)

    def tiled(matrix):
        return jnp.concatenate([matrix] * 4, axis=1)

    own, out, mix, own_back, out_back, mix_back = [2 * at for at in range(6)]
    entry = [jnp.concatenate([edge_in_ref[layer][:, :F], edge_in_ref[layer][:, F:]], axis=0) for layer in range(2)]
    build_hot(hot_target, target_of)
    sums = edge_forward(0, times(spread(entry[0]), x_ref[...]))
    ship(0, at_slots(sums))
    rim_counts = [f + r for f, r in counts]
    present = jnp.int32(rim_counts[0])
    for rim in range(1, 4):
        present = jnp.where(at_rim == rim, rim_counts[rim], present)
    pl.semaphore_wait(barrier, present)
    send(0)

    for layer in range(2):
        node = node_in_ref[layer]
        mixed = times(spread(node[:, F:]), tiled(edge_out_ref[layer]))[:, :F]
        small_to[own + layer] = spread(node[:, :F])
        small_to[out + layer] = spread(node_out_ref[layer])
        small_to[mix + layer] = spread(mixed)
        small_to[own_back + layer] = spread_flipped(node[:, :F])
        small_to[out_back + layer] = spread_flipped(node_out_ref[layer])
        small_to[mix_back + layer] = spread_flipped(mixed)
        ends_from[layer] = spread_flipped(entry[layer])
    ends_to[0] = spread(entry[1])
    through = times(ends_to[0], tiled(node_out_ref[0]))[:, :F]
    ends_to[1] = spread(through)
    ends_from[2] = spread_flipped(through)
    codes = node_slots()
    build_hot(hot_source, source_of)
    held[4] = slope_sums(0)
    field = x_ref[...]
    held[0] = times(small_to[own], field)
    both_ends = times(ends_to[0], field)
    held[5] = both_ends[:F]
    held[6] = both_ends[F:]
    receive(0)
    pre = held[0] + times(small_to[mix], sums + unpack(0, codes))
    gate = sigmoid_of(pre)
    active = pre * gate
    held[7] = gate * (1.0 + pre * (1.0 - gate))
    table = jnp.concatenate([held[5], held[6]], axis=0) + times(ends_to[1], active)
    sums = edge_forward(1, table)
    ship(1, at_slots(sums))
    send(1)
    field = field + times(small_to[out], active)
    held[1] = times(small_to[own + 1], field)
    held[8] = times(small_to[out_back + 1], cot_ref[...])
    held[5] = slope_sums(1)
    local = held[1] + times(small_to[mix + 1], sums)
    held[9] = at_slots(local)
    held[10] = at_slots(held[8])
    receive(1)
    arrived = arrivals(1)
    arrived = jnp.concatenate([arrived[F * g : F * g + F] for g in range(4)], axis=1)
    pre = held[9] + times(small_to[mix + 1], arrived)
    gate = sigmoid_of(pre)
    delta = held[10] * (gate * (1.0 + pre * (1.0 - gate)))
    ship(2, times(small_to[mix_back + 1], delta))
    send(2)
    pre = held[1] + times(small_to[mix + 1], sums + unpack(1, codes))
    gate = sigmoid_of(pre)
    delta = held[8] * (gate * (1.0 + pre * (1.0 - gate)))
    sums = times(small_to[mix_back + 1], delta)
    updated_ref[...] = field + times(small_to[out + 1], pre * gate)
    held[2] = cot_ref[...] + times(small_to[own_back + 1], delta)
    held[6] = times(small_to[out_back], held[2])
    receive(2)
    both = edge_backward(1, sums + unpack(2, codes), held[5])
    delta = (held[6] + times(ends_from[2], both)) * held[7]
    sums = times(small_to[mix_back], delta)
    ship(3, at_slots(sums))
    send(3)
    held[3] = held[2] + times(ends_from[1], both) + times(small_to[own_back], delta)
    receive(3)
    both = edge_backward(0, sums + unpack(3, codes), held[4])
    grad_ref[...] = held[3] + times(ends_from[0], both)

    for rim, (faces, rims) in enumerate(counts):

        @pl.when(at_rim == rim)
        def _():
            for block, which in ((face_out.at[:, 0:faces], 0), (rim_out.at[:, 0:rims], 1)):
                pltpu.make_async_copy(block, block, send_sem.at[which]).wait()


def solution(mesh):
    sizes = tuple(mesh.shape[axis] for axis in AXES)

    def on_device(*operands):
        nodes = operands[0].shape[1]
        edges = operands[1].shape[1]
        anywhere = pl.BlockSpec(memory_space=pl.ANY)
        vmem = pl.BlockSpec(memory_space=pltpu.VMEM)
        results = pl.pallas_call(
            functools.partial(kernel, sizes),
            out_shape=(pltpu.VMEM((F, nodes), f32), pltpu.VMEM((F, nodes), f32)),
            in_specs=[anywhere] * len(operands),
            out_specs=(vmem, vmem),
            scratch_shapes=[
                *(pltpu.VMEM(operand.shape, operand.dtype) for operand in operands),
                pltpu.SemaphoreType.DMA((len(operands),)),
                pltpu.VMEM((256, edges), bf16),
                pltpu.VMEM((256, edges), bf16),
                pltpu.VMEM((2, F, edges), f32),
                pltpu.VMEM((128, edges), bf16),
                pltpu.VMEM((LANES, LANES), i32),
                pltpu.VMEM((11, F, nodes), f32),
                pltpu.VMEM((2, 2 * F, LANES), bf16),
                pltpu.VMEM((12, F, LANES), bf16),
                pltpu.VMEM((3, F, 2 * LANES), bf16),
                pltpu.VMEM((4, len(FACES), 8, LANES), f32),
                pltpu.VMEM((4, 27, 1, LANES), f32),
                pltpu.VMEM((4, len(FACES), 8, LANES), f32),
                pltpu.VMEM((4, 27, 1, LANES), f32),
                pltpu.SemaphoreType.DMA((2,)),
                pltpu.SemaphoreType.DMA((4, 2)),
            ],
            compiler_params=pltpu.CompilerParams(collective_id=0, has_side_effects=True),
        )(*operands)

        def store(updated_ref, grad_ref, updated_out, grad_out, sems):
            copies = [
                pltpu.make_async_copy(updated_ref, updated_out, sems.at[0]),
                pltpu.make_async_copy(grad_ref, grad_out, sems.at[1]),
            ]
            for copy in copies:
                copy.start()
            for copy in copies:
                copy.wait()

        return pl.pallas_call(
            store,
            out_shape=(jax.ShapeDtypeStruct((F, nodes), f32), jax.ShapeDtypeStruct((F, nodes), f32)),
            in_specs=[vmem, vmem],
            out_specs=(anywhere, anywhere),
            scratch_shapes=[pltpu.SemaphoreType.DMA((2,))],
        )(*[pltpu.with_memory_space_constraint(result, pltpu.VMEM) for result in results])

    split_columns = P(None, AXES)
    return jax.shard_map(
        on_device,
        mesh=mesh,
        in_specs=(split_columns, split_columns, split_columns, P(), P(), P(), P(), split_columns),
        out_specs=(split_columns, split_columns),
        check_vma=False,
    )
```
